256 devices in a mesh: dp: 8 (over y, z_hi), ctx: 32 (over z_lo, x, core).
Axes of the slice: x: 4, y: 4, z: 8 (z_hi: 2, z_lo: 4; z = z_hi * 4 + z_lo), core: 2. Of those that a mesh axis runs over, the one named last changes fastest.
Arguments:
- layer_input: bfloat16 [8, 4096, 3072], P('dp', 'ctx'), may hold values from -6 to 6
- query_rows: bfloat16 [8, 4096, 3072], P('dp', 'ctx'), may hold values from -6 to 6
- key_rows: bfloat16 [8, 4096, 3072], P('dp', 'ctx'), may hold values from -6 to 6
- value_rows: bfloat16 [8, 4096, 3072], P('dp', 'ctx'), may hold values from -6 to 6
- out_grad: bfloat16 [8, 4096, 3072], P('dp', 'ctx'), may hold values from -6 to 6
Outputs:
- query_grad: bfloat16 [8, 4096, 3072], P('dp', 'ctx')
- key_grad: bfloat16 [8, 4096, 3072], P('dp', 'ctx')
- value_grad: bfloat16 [8, 4096, 3072], P('dp', 'ctx')
- key_weight_grad: float32 [3072, 3072], P('ctx', 'dp')
The draws below stay inside these ranges and needn't reach their ends.
All inputs are finite; a program needn't handle non-finite values.
Results may differ from the reference program's by a relative error of at most 0.028.
Values may be sent and summed in bfloat16 or wider, within the bound.
A program may use at most 192 MiB of HBM per device.

```python
import jax
import jax.numpy as jnp
from jax import lax

DW = 3072
HEADS = 24
HEAD_DIM = 128
TOK_DEV = 128
HD = 3072
SEQS = 8
LENGTH = 4096
N_CTX = 32


def level_of(key, dims, shards, smallest, high):
    level = 1.0
    for axis_at, parts in shards:
        draws = jax.random.uniform(jax.random.fold_in(jax.random.fold_in(key, 6), axis_at), (parts,), jnp.float32, smallest / len(shards), high / len(shards))
        level = level * jnp.repeat(jnp.exp(draws), dims[axis_at] // parts).reshape((-1,) + (1,) * (len(dims) - 1 - axis_at))
    return level


def bell_draw(own_key, shape, scale, bound, cuts=(), held_as=jnp.bfloat16):
    values = jax.random.normal(own_key, shape, jnp.float32) * scale
    if len(cuts) > 0:
        values = level_of(own_key, shape, cuts, -0.22, 0.18) * values
    return jnp.clip(values, min=-bound, max=bound).astype(held_as)


def setup_inputs(seed: int = 0) -> dict:
    arg_keys = jax.random.split(jax.random.key(seed), 6)
    layer_input = bell_draw(arg_keys[0], (SEQS, LENGTH, DW), 1.0, 6.0, ((0, 8), (1, 32)))
    query_rows = bell_draw(arg_keys[1], (SEQS, LENGTH, HD), 1.0, 6.0, ((0, 8), (1, 32)))
    key_rows = bell_draw(arg_keys[2], (SEQS, LENGTH, HD), 1.0, 6.0, ((0, 8), (1, 32)))
    value_rows = bell_draw(arg_keys[3], (SEQS, LENGTH, HD), 1.0, 6.0, ((0, 8), (1, 32)))
    out_grad = bell_draw(arg_keys[4], (SEQS, LENGTH, HD), 1.0, 6.0, ((0, 8), (1, 32)))
    return {"layer_input": layer_input, "query_rows": query_rows, "key_rows": key_rows, "value_rows": value_rows, "out_grad": out_grad}


epsilon = 1e-05

def feature(values):
    wide = values.astype(jnp.float32)
    return jax.nn.elu(wide) + 1.0

def slope(values):
    wide = values.astype(jnp.float32)
    return jnp.where(wide > 0, 1.0, jnp.exp(jnp.minimum(wide, 0.0)))

def round_half(values):
    return lax.optimization_barrier(values.astype(jnp.bfloat16)).astype(jnp.float32)

def one_sequence(operands):
    query_rows, key_rows, value_rows, out_grad = operands
    shaped = (N_CTX, TOK_DEV, HEADS, HEAD_DIM)
    query = query_rows.reshape(shaped)
    keyed = key_rows.reshape(shaped)
    query_feature = round_half(feature(query))
    key_feature = round_half(feature(keyed))
    values = value_rows.reshape(shaped).astype(jnp.float32)
    upstream = out_grad.reshape(shaped).astype(jnp.float32)
    rows_index = lax.broadcasted_iota(jnp.int32, (TOK_DEV, TOK_DEV), 0)
    cols_index = lax.broadcasted_iota(jnp.int32, (TOK_DEV, TOK_DEV), 1)
    causal = (cols_index <= rows_index)[None, None]
    block_state = jnp.einsum('nthd,nthe->nhde', key_feature, values)
    prefix = jnp.cumsum(block_state, axis=0)
    state_in = round_half(jnp.concatenate([jnp.zeros_like(block_state[:1]), prefix[:-1]], axis=0))
    scores = jnp.einsum('nthd,nshd->nhts', query_feature, key_feature)
    scores = round_half(jnp.where(causal, scores, 0.0))
    output = jnp.einsum('nhts,nshe->nthe', scores, values) + jnp.einsum('nthd,nhde->nthe', query_feature, state_in)
    inverse_rms = lax.rsqrt(lax.optimization_barrier(jnp.mean(output * output, axis=-1, keepdims=True)) + epsilon)
    normed = output * inverse_rms
    projection = lax.optimization_barrier(jnp.mean(upstream * normed, axis=-1, keepdims=True))
    grad_output = round_half(inverse_rms * (upstream - normed * projection))
    block_grad = jnp.einsum('nthd,nthe->nhde', query_feature, grad_output)
    suffix = jnp.cumsum(block_grad[::-1], axis=0)[::-1]
    grad_in = round_half(jnp.concatenate([suffix[1:], jnp.zeros_like(block_grad[:1])], axis=0))
    grad_scores = jnp.einsum('nthe,nshe->nhts', grad_output, values)
    grad_scores = round_half(jnp.where(causal, grad_scores, 0.0))
    query_total = jnp.einsum('nhts,nshd->nthd', grad_scores, key_feature) + jnp.einsum('nthe,nhde->nthd', grad_output, state_in)
    key_total = jnp.einsum('nhts,nthd->nshd', grad_scores, query_feature) + jnp.einsum('nshe,nhde->nshd', values, grad_in)
    value_total = jnp.einsum('nhts,nthe->nshe', scores, grad_output) + jnp.einsum('nshd,nhde->nshe', key_feature, grad_in)
    query_grad = (query_total * slope(query)).astype(jnp.bfloat16).reshape(LENGTH, HD)
    key_grad = (key_total * slope(keyed)).astype(jnp.bfloat16).reshape(LENGTH, HD)
    value_grad = value_total.astype(jnp.bfloat16).reshape(LENGTH, HD)
    return (query_grad, key_grad, value_grad)

def reference(layer_input, query_rows, key_rows, value_rows, out_grad):
    query_grad, key_grad, value_grad = lax.map(one_sequence, (query_rows, key_rows, value_rows, out_grad))
    blocks_key = key_grad.reshape(SEQS * N_CTX, TOK_DEV, HD)
    blocks_input = layer_input.reshape(SEQS * N_CTX, TOK_DEV, DW)
    scale = (SEQS * LENGTH) ** (-0.5)

    def add_block(total, pair):
        piece = jnp.dot(pair[0].T, pair[1], preferred_element_type=jnp.float32)
        return (total + round_half(piece), None)
    result = lax.scan(add_block, jnp.zeros((HD, DW), jnp.float32), (blocks_key, blocks_input))
    weight_grad = result[0] * scale
    return (query_grad, key_grad, value_grad, weight_grad)
```

```python
import functools

import jax
import jax.numpy as jnp
from jax import lax
from jax.experimental import pallas as pl
from jax.experimental.pallas import tpu as pltpu
from jax.sharding import PartitionSpec as P

HEADS = 24
HD = 128
TOK = 128
HALF = 12
CHIPS = 16
PIECE = 96
WIDE = 3072
EPS = 1e-05
SCALE = (8 * 32 * 128) ** (-0.5)
MESH = pl.DeviceIdType.MESH
F32 = jnp.float32
BF16 = jnp.bfloat16
GROUP = 4

NN = (((1,), (0,)), ((), ()))
NT = (((1,), (1,)), ((), ()))
TN = (((0,), (0,)), ((), ()))


def mm(a, b, dims):
    return lax.dot_general(a, b, dims, preferred_element_type=F32)


def feature(x):
    return jnp.where(x > 0, x + 1.0, jnp.exp(jnp.minimum(x, 0.0)))


def slope(x):
    return jnp.where(x > 0, 1.0, jnp.exp(jnp.minimum(x, 0.0)))


def cols(h):
    return pl.ds(pl.multiple_of(h * HD, HD), HD)


def kernel(
    x_ref, q_ref, k_ref, v_ref, og_ref,
    dq_out, dk_out, dv_out, dw_out,
    qf, kf, go, ol, dkl, dvl, sc,
    st, pb, cs, r1, ex, pr, po, si,
    dq, dk, dv, kgt, xb, at, cp, xr, zs, zr, tb, tr,
    pair_s, pair_r, a2a_s, a2a_r, xb_s, xb_r, at_s, at_r,
    cx_s, cx_r, z_s, z_r, t_s, t_r, loc,
):
    d = lax.axis_index("dp")
    c = lax.axis_index("ctx")
    y, zh = d // 2, d % 2
    chip, core = c // 2, c % 2
    zl, x = chip // 4, chip % 4
    other = 1 - core

    def dev(y_, zh_, zl_, x_, core_):
        return (y_ * 2 + zh_, (zl_ * 4 + x_) * 2 + core_)

    partner = (d, chip * 2 + other)

    def remote(src, dst, ss, rs, to):
        return pltpu.make_async_remote_copy(
            src_ref=src, dst_ref=dst, send_sem=ss, recv_sem=rs,
            device_id=to, device_id_type=MESH,
        )

    barrier = pltpu.get_barrier_semaphore()

    def greet(to):
        pl.semaphore_signal(barrier, inc=1, device_id=to, device_id_type=MESH)

    greet(partner)
    for o in range(1, CHIPS):
        greet((d, ((chip + o) % CHIPS) * 2 + core))
    for o in range(1, 4):
        for cc in (0, 1):
            greet(dev((y + o) % 4, zh, zl, x, cc))
    for o in range(4):
        greet(dev(y, 1 - zh, o, x, core))
    flip = dev(zl, zh, y, x, core)
    off = y != zl

    @pl.when(off)
    def _():
        greet(flip)

    row = lax.broadcasted_iota(jnp.int32, (TOK, TOK), 0)
    col = lax.broadcasted_iota(jnp.int32, (TOK, TOK), 1)
    causal = col <= row

    def heads(first, count, body):
        def step(g, carry):
            for j in range(GROUP):
                body(first + g * GROUP + j)
            return carry

        lax.fori_loop(0, count // GROUP, step, 0)

    def states(h):
        at_h = cols(h)
        kfh = feature(k_ref[:, at_h].astype(F32)).astype(BF16)
        qf[:, at_h] = feature(q_ref[:, at_h].astype(F32)).astype(BF16)
        kf[:, at_h] = kfh
        st[0, h] = mm(kfh, v_ref[:, at_h], TN).astype(BF16)

    heads(HALF * other, HALF, states)

    pl.semaphore_wait(barrier, 26 + ((y - zl) * (y - zl) + 8) // 9)

    def pair_out(s):
        return remote(
            st.at[s, pl.ds(HALF * other, HALF)], pb.at[s],
            pair_s.at[2 * s], pair_r.at[2 * s], partner,
        )

    def pair_back(s):
        return remote(
            po.at[s], si.at[s, pl.ds(HALF * core, HALF)],
            pair_s.at[2 * s + 1], pair_r.at[2 * s + 1], partner,
        )

    def pair_back_in(s):
        return remote(
            po.at[s], si.at[s, pl.ds(HALF * other, HALF)],
            pair_s.at[2 * s + 1], pair_r.at[2 * s + 1], partner,
        )

    def toward(s, o):
        to = (chip + o) % CHIPS
        return remote(
            cs.at[s, pl.ds(PIECE * to, PIECE)], r1.at[s, chip],
            a2a_s.at[2 * s, o], a2a_r.at[2 * s, o], (d, to * 2 + core),
        )

    def toward_in(s, o):
        src = (chip + CHIPS - o) % CHIPS
        return remote(
            cs.at[s, pl.ds(PIECE * src, PIECE)], r1.at[s, src],
            a2a_s.at[2 * s, o], a2a_r.at[2 * s, o], (d, src * 2 + core),
        )

    def away(s, o):
        to = (chip + o) % CHIPS
        return remote(
            ex.at[s, to], pr.at[s, pl.ds(PIECE * chip, PIECE)],
            a2a_s.at[2 * s + 1, o], a2a_r.at[2 * s + 1, o], (d, to * 2 + core),
        )

    def away_in(s, o):
        src = (chip + CHIPS - o) % CHIPS
        return remote(
            ex.at[s, src], pr.at[s, pl.ds(PIECE * src, PIECE)],
            a2a_s.at[2 * s + 1, o], a2a_r.at[2 * s + 1, o], (d, src * 2 + core),
        )

    def scan(s, meanwhile):
        pair_out(s).wait_recv()

        def add(i, carry):
            both = st[s, HALF * core + i].astype(F32) + pb[s, i].astype(F32)
            cs[s, pl.ds(pl.multiple_of(i * HD, HD), HD), :] = both.astype(BF16)
            return carry

        lax.fori_loop(0, HALF, add, 0)
        for o in range(1, CHIPS):
            toward(s, o).start()
        r1[s, chip] = cs[s, pl.ds(pl.multiple_of(PIECE * chip, PIECE), PIECE), :]
        meanwhile()
        for o in range(1, CHIPS):
            toward_in(s, o).wait_recv()
        total = jnp.zeros((PIECE, HD), F32)
        for i in range(CHIPS):
            n = i if s == 0 else CHIPS - 1 - i
            ex[s, n] = total.astype(BF16)
            total = total + r1[s, n].astype(F32)
        for o in range(1, CHIPS):
            away(s, o).start()
        pr[s, pl.ds(pl.multiple_of(PIECE * chip, PIECE), PIECE), :] = ex[s, chip]

    def finish(s):
        for o in range(1, CHIPS):
            away_in(s, o).wait_recv()
        mine_on = (core if s == 0 else 1 - core).astype(F32)
        theirs_on = 1.0 - mine_on

        def theirs(i, carry):
            base = pr[s, pl.ds(pl.multiple_of(i * HD, HD), HD), :].astype(F32)
            po[s, i] = (base + theirs_on * st[s, HALF * core + i].astype(F32)).astype(BF16)
            return carry

        lax.fori_loop(0, HALF, theirs, 0)
        pair_back(s).start()

        def mine(i, carry):
            base = pr[s, pl.ds(pl.multiple_of(i * HD, HD), HD), :].astype(F32)
            si[s, HALF * core + i] = (base + mine_on * pb[s, i].astype(F32)).astype(BF16)
            return carry

        lax.fori_loop(0, HALF, mine, 0)

    slot = 2 * y + core

    def xrows(n):
        return pl.ds(pl.multiple_of(TOK * n, TOK), TOK)

    pair_out(0).start()
    own_x = pltpu.make_async_copy(x_ref, xb.at[xrows(slot)], loc.at[0])
    own_x.start()

    def x_send(o):
        return remote(
            x_ref, xb.at[xrows(slot)], xb_s.at[o], xb_r.at[o],
            dev((y + o) % 4, zh, zl, x, core),
        )

    def x_in(o):
        src = (y + 4 - o) % 4
        return remote(
            x_ref, xb.at[xrows(2 * src + core)], xb_s.at[o], xb_r.at[o],
            dev(src, zh, zl, x, core),
        )

    def x_pass(o):
        src = (y + 4 - o) % 4
        rows = xb.at[xrows(2 * src + core)]
        return remote(rows, rows, xb_s.at[4 + o], xb_r.at[4 + o], partner)

    def x_pass_in(o):
        src = (y + 4 - o) % 4
        rows = xb.at[xrows(2 * src + other)]
        return remote(rows, rows, xb_s.at[4 + o], xb_r.at[4 + o], partner)

    x_keep = remote(x_ref, xb.at[xrows(slot)], xb_s.at[4], xb_r.at[4], partner)
    x_keep_in = remote(x_ref, xb.at[xrows(2 * y + other)], xb_s.at[4], xb_r.at[4], partner)

    for o in (1, 3, 2):
        x_send(o).start()

    heads(HALF * core, HALF, states)

    def local_out(h):
        at_h = cols(h)
        s_h = mm(qf[:, at_h], kf[:, at_h], NT)
        s_h = jnp.where(causal, s_h, 0.0).astype(BF16)
        sc[h] = s_h
        ol[:, at_h] = mm(s_h, v_ref[:, at_h], NN)

    scan(0, lambda: heads(0, HEADS, local_out))
    finish(0)
    x_keep.start()

    def grads(h):
        at_h = cols(h)
        out = ol[:, at_h] + mm(qf[:, at_h], si[0, h], NN)
        inv = lax.rsqrt(jnp.mean(out * out, axis=-1, keepdims=True) + EPS)
        normed = out * inv
        up = og_ref[:, at_h].astype(F32)
        proj = jnp.mean(up * normed, axis=-1, keepdims=True)
        g_h = (inv * (up - normed * proj)).astype(BF16)
        go[:, at_h] = g_h
        st[1, h] = mm(qf[:, at_h], g_h, TN).astype(BF16)

    pair_back_in(0).wait_recv()
    heads(HALF * other, HALF, grads)
    pair_out(1).start()
    heads(HALF * core, HALF, grads)

    def local_grads(h):
        at_h = cols(h)
        g_h = go[:, at_h]
        gs = mm(g_h, v_ref[:, at_h], NT)
        gs = jnp.where(causal, gs, 0.0).astype(BF16)
        total = mm(gs, kf[:, at_h], NN) + mm(g_h, si[0, h], NT)
        dq[:, at_h] = (total * slope(q_ref[:, at_h].astype(F32))).astype(BF16)
        dkl[:, at_h] = mm(gs, qf[:, at_h], TN)
        dvl[:, at_h] = mm(sc[h], g_h, TN)

    def during():
        for o in (1, 3, 2):
            x_in(o).wait_recv()
            x_pass(o).start()
        heads(0, HEADS, local_grads)

    scan(1, during)
    out_q = pltpu.make_async_copy(dq, dq_out, loc.at[1])
    out_q.start()
    finish(1)
    pair_back_in(1).wait_recv()

    def last(h):
        at_h = cols(h)
        gi = si[1, h]
        total = dkl[:, at_h] + mm(v_ref[:, at_h], gi, NT)
        total = total * slope(k_ref[:, at_h].astype(F32))
        dk[:, at_h] = total.astype(BF16)
        kgt[pl.ds(pl.multiple_of(h * HD, HD), HD), :] = total.T.astype(BF16)
        dv[:, at_h] = (dvl[:, at_h] + mm(kf[:, at_h], gi, NN)).astype(BF16)

    heads(0, HEADS, last)

    def at_rows(y_, core_, n):
        return kgt.at[pl.ds(pl.multiple_of(768 * y_ + 192 * n + 96 * core_, 96), 96)]

    def at_put(src, n):
        return at.at[pl.ds(96 * n, 96), pl.ds(pl.multiple_of(TOK * src, TOK), TOK)]

    def at_send(o, cc, n):
        y_ = (y + o) % 4
        cc_ = (core + cc) % 2
        return remote(
            at_rows(y_, cc_, n), at_put(slot, n), at_s.at[2 * o + cc, n], at_r.at[2 * o + cc, n],
            dev(y_, zh, zl, x, cc_),
        )

    def at_in(o, cc, n):
        y_ = (y + 4 - o) % 4
        cc_ = (core + cc) % 2
        return remote(
            at_rows(y, core, n), at_put(2 * y_ + cc_, n), at_s.at[2 * o + cc, n], at_r.at[2 * o + cc, n],
            dev(y_, zh, zl, x, cc_),
        )

    peers = [(o, cc) for o in (2, 1, 3, 0) for cc in (0, 1) if (o, cc) != (0, 0)]
    for o, cc in peers:
        for n in range(4):
            at_send(o, cc, n).start()
    for n in range(4):
        keep = pltpu.make_async_copy(at_rows(y, core, n), at_put(slot, n), loc.at[4 + n])
        keep.start()
    out_k = pltpu.make_async_copy(dk, dk_out, loc.at[2])
    out_v = pltpu.make_async_copy(dv, dv_out, loc.at[3])
    out_k.start()
    out_v.start()

    own_x.wait()
    x_keep_in.wait_recv()
    for o in (1, 3, 2):
        x_pass_in(o).wait_recv()
    for n in range(4):
        pltpu.make_async_copy(at_rows(y, core, n), at_put(slot, n), loc.at[4 + n]).wait()
        for o, cc in peers:
            at_in(o, cc, n).wait_recv()

    def cx_send(o):
        to = (x + o) % 4
        return remote(cp.at[to], xr.at[x], cx_s.at[o], cx_r.at[o], dev(y, zh, zl, to, core))

    def cx_in(o):
        src = (x + 4 - o) % 4
        return remote(cp.at[src], xr.at[src], cx_s.at[o], cx_r.at[o], dev(y, zh, zl, src, core))

    def product(n, carry):
        tile = mm(at[...], xb[:, pl.ds(pl.multiple_of(n * 384, 384), 384)], NN).astype(BF16)
        for i in range(4):
            cp[i, n] = tile[96 * i:96 * (i + 1), :]
        return carry

    lax.fori_loop(0, 8, product, 0)
    for o in (2, 1, 3):
        cx_send(o).start()
    for o in (1, 3, 2):
        cx_in(o).wait_recv()

    def sum_x(n, carry):
        total = cp[x, n].astype(F32)
        for o in range(1, 4):
            total = total + xr[(x + o) % 4, n].astype(F32)
        zs[n] = total.astype(BF16)
        return carry

    lax.fori_loop(0, 8, sum_x, 0)

    z = zh * 4 + zl

    def z_send(o):
        to = (z + o) % 8
        return remote(
            zs.at[(to % 4) * 2 + to // 4], zr.at[o], z_s.at[o], z_r.at[o],
            dev(y, to // 4, to % 4, x, core),
        )

    def z_in(o):
        src = (z + 8 - o) % 8
        return remote(
            zs.at[(src % 4) * 2 + src // 4], zr.at[o], z_s.at[o], z_r.at[o],
            dev(y, src // 4, src % 4, x, core),
        )

    for o in (4, 3, 5, 2, 6, 1, 7):
        z_send(o).start()
    for o in range(1, 8):
        z_in(o).wait_recv()
    total = zs[zl * 2 + zh].astype(F32)
    for o in range(1, 8):
        total = total + zr[o].astype(F32)
    tb[...] = total.astype(BF16)

    turn = remote(tb, tr, t_s.at[0], t_r.at[0], flip)

    @pl.when(off)
    def _():
        turn.start()
        turn.wait()
        dw_out[...] = tr[...].astype(F32) * SCALE

    @pl.when(jnp.logical_not(off))
    def _():
        dw_out[...] = tb[...].astype(F32) * SCALE

    for s in (0, 1):
        pair_out(s).wait_send()
        pair_back(s).wait_send()
        for o in range(1, CHIPS):
            toward(s, o).wait_send()
            away(s, o).wait_send()
    for o in (1, 3, 2):
        x_send(o).wait_send()
        x_pass(o).wait_send()
        cx_send(o).wait_send()
    x_keep.wait_send()
    for o, cc in peers:
        for n in range(4):
            at_send(o, cc, n).wait_send()
    for o in range(1, 8):
        z_send(o).wait_send()
    out_q.wait()
    out_k.wait()
    out_v.wait()


def shards(layer_input, query_rows, key_rows, value_rows, out_grad):
    vmem = pl.BlockSpec(memory_space=pltpu.VMEM)
    hbm = pl.BlockSpec(memory_space=pl.ANY)
    rows = (TOK, WIDE)
    state = (HALF, HD, HD)
    dma = pltpu.SemaphoreType.DMA
    dq, dk, dv, dw = pl.pallas_call(
        kernel,
        out_shape=(
            jax.ShapeDtypeStruct(rows, BF16),
            jax.ShapeDtypeStruct(rows, BF16),
            jax.ShapeDtypeStruct(rows, BF16),
            jax.ShapeDtypeStruct((96, 384), F32),
        ),
        in_specs=[hbm, vmem, vmem, vmem, vmem],
        out_specs=(hbm, hbm, hbm, vmem),
        scratch_shapes=[
            pltpu.VMEM(rows, BF16),
            pltpu.VMEM(rows, BF16),
            pltpu.VMEM(rows, BF16),
            pltpu.VMEM(rows, F32),
            pltpu.VMEM(rows, F32),
            pltpu.VMEM(rows, F32),
            pltpu.VMEM((HEADS, HD, HD), BF16),
            pltpu.VMEM((2, HEADS, HD, HD), BF16),
            pltpu.VMEM((2,) + state, BF16),
            pltpu.VMEM((2, HALF * HD, HD), BF16),
            pltpu.VMEM((2, CHIPS, PIECE, HD), BF16),
            pltpu.VMEM((2, CHIPS, PIECE, HD), BF16),
            pltpu.VMEM((2, HALF * HD, HD), BF16),
            pltpu.VMEM((2,) + state, BF16),
            pltpu.VMEM((2, HEADS, HD, HD), BF16),
            pltpu.VMEM(rows, BF16),
            pltpu.VMEM(rows, BF16),
            pltpu.VMEM(rows, BF16),
            pltpu.VMEM((WIDE, TOK), BF16),
            pltpu.VMEM((8 * TOK, WIDE), BF16),
            pltpu.VMEM((384, 8 * TOK), BF16),
            pltpu.VMEM((4, 8, 96, 384), BF16),
            pltpu.VMEM((4, 8, 96, 384), BF16),
            pltpu.VMEM((8, 96, 384), BF16),
            pltpu.VMEM((8, 96, 384), BF16),
            pltpu.VMEM((96, 384), BF16),
            pltpu.VMEM((96, 384), BF16),
            dma((4,)), dma((4,)),
            dma((4, CHIPS)), dma((4, CHIPS)),
            dma((8,)), dma((8,)),
            dma((8, 4)), dma((8, 4)),
            dma((4,)), dma((4,)),
            dma((8,)), dma((8,)),
            dma((1,)), dma((1,)),
            dma((8,)),
        ],
        compiler_params=pltpu.CompilerParams(
            collective_id=0, has_side_effects=True, vmem_limit_bytes=60 * 1024 * 1024
        ),
    )(layer_input[0], query_rows[0], key_rows[0], value_rows[0], out_grad[0])
    return dq[None], dk[None], dv[None], dw


def solution(mesh):
    placed = (P("dp", "ctx", None),) * 5
    return jax.shard_map(
        shards,
        mesh=mesh,
        in_specs=placed,
        out_specs=(
            P("dp", "ctx", None),
            P("dp", "ctx", None),
            P("dp", "ctx", None),
            P("ctx", "dp"),
        ),
        check_vma=False,
    )
```

```python
import functools

import jax
import jax.numpy as jnp
from jax import lax
from jax.experimental import pallas as pl
from jax.experimental.pallas import tpu as pltpu
from jax.sharding import PartitionSpec as P

HEADS = 24
HD = 128
TOK = 128
CHUNKS = 3
PART = 4
SPAN = 8
WIDE = 3072
EPS = 1e-05
SCALE = (8 * 32 * 128) ** (-0.5)
MESH = pl.DeviceIdType.MESH
F32 = jnp.float32
BF16 = jnp.bfloat16
GROUP = 4

NN = (((1,), (0,)), ((), ()))
NT = (((1,), (1,)), ((), ()))
TN = (((0,), (0,)), ((), ()))


def mm(a, b, dims):
    return lax.dot_general(a, b, dims, preferred_element_type=F32)


def feature(x):
    return jnp.where(x > 0, x + 1.0, jnp.exp(jnp.minimum(x, 0.0)))


def slope(x):
    return jnp.where(x > 0, 1.0, jnp.exp(jnp.minimum(x, 0.0)))


def cols(h):
    return pl.ds(pl.multiple_of(h * HD, HD), HD)


def kernel(
    x_ref, q_ref, k_ref, v_ref, og_ref,
    dq_out, dk_out, dv_out, dw_out,
    qf, kf, go, ol, dkl, dvl, sc,
    st, pb, cs, r1, rt, rz, ex, pr, po, si,
    dq, dk, dv, kgt, xb, at, cp, xr, zs, zr, tb, tr,
    pair_s, pair_r, in_s, in_r, row_s, row_r, back_s, back_r,
    xb_s, xb_r, at_s, at_r, cx_s, cx_r, z_s, z_r, t_s, t_r, loc,
):
    d = lax.axis_index("dp")
    c = lax.axis_index("ctx")
    y, zh = d // 2, d % 2
    chip, core = c // 2, c % 2
    zl, x = chip // 4, chip % 4
    other = 1 - core

    def dev(y_, zh_, zl_, x_, core_):
        return (y_ * 2 + zh_, (zl_ * 4 + x_) * 2 + core_)

    partner = (d, chip * 2 + other)

    def remote(src, dst, ss, rs, to):
        return pltpu.make_async_remote_copy(
            src_ref=src, dst_ref=dst, send_sem=ss, recv_sem=rs,
            device_id=to, device_id_type=MESH,
        )

    barrier = pltpu.get_barrier_semaphore()

    def greet(to):
        pl.semaphore_signal(barrier, inc=1, device_id=to, device_id_type=MESH)

    greet(partner)
    for o in range(1, 4):
        greet(dev(y, zh, zl, (x + o) % 4, core))
        greet(dev(y, zh, (zl + o) % 4, x, core))
        for cc in (0, 1):
            greet(dev((y + o) % 4, zh, zl, x, cc))
    for o in range(4):
        greet(dev(y, 1 - zh, o, x, core))
    flip = dev(zl, zh, y, x, core)
    off = y != zl

    @pl.when(off)
    def _():
        greet(flip)

    row = lax.broadcasted_iota(jnp.int32, (TOK, TOK), 0)
    col = lax.broadcasted_iota(jnp.int32, (TOK, TOK), 1)
    causal = col <= row

    def heads(k, body):
        def step(g, carry):
            for j in range(GROUP):
                body(SPAN * k + g * GROUP + j)
            return carry

        lax.fori_loop(0, SPAN // GROUP, step, 0)

    def states(h):
        at_h = cols(h)
        kfh = feature(k_ref[:, at_h].astype(F32)).astype(BF16)
        qf[:, at_h] = feature(q_ref[:, at_h].astype(F32)).astype(BF16)
        kf[:, at_h] = kfh
        st[0, h] = mm(kfh, v_ref[:, at_h], TN).astype(BF16)

    def pair_out(s, k):
        return remote(
            st.at[s, pl.ds(SPAN * k + PART * other, PART)], pb.at[s, k],
            pair_s.at[s, 0, k], pair_r.at[s, 0, k], partner,
        )

    def pair_back(s, k, who):
        return remote(
            po.at[s, k], si.at[s, pl.ds(SPAN * k + PART * who, PART)],
            pair_s.at[s, 1, k], pair_r.at[s, 1, k], partner,
        )

    def ahead(o):
        return (x + o) % 4

    def behind(o):
        return (x + 4 - o) % 4

    def x_peer(n):
        return dev(y, zh, zl, n, core)

    def enter(s, k, o, source, slot_, peer):
        return remote(
            cs.at[s, k, source], r1.at[s, k, slot_],
            in_s.at[s, k, o], in_r.at[s, k, o], x_peer(peer),
        )

    def along(s, k, o, slot_, peer):
        return remote(
            rt.at[s, k], rz.at[s, k, slot_],
            row_s.at[s, k, o], row_r.at[s, k, o], dev(y, zh, peer, x, core),
        )

    def leave(s, k, o, source, slot_, peer):
        return remote(
            ex.at[s, k, source], pr.at[s, k, slot_],
            back_s.at[s, k, o], back_r.at[s, k, o], x_peer(peer),
        )

    FAR = (2, 1, 3)

    def stage1(s, k):
        pair_out(s, k).wait_recv()
        for j in range(PART):
            both = st[s, SPAN * k + PART * core + j].astype(F32) + pb[s, k, j].astype(F32)
            cs[s, k, j] = both.astype(BF16)
        for o in FAR:
            enter(s, k, o, ahead(o), x, ahead(o)).start()
        r1[s, k, x] = cs[s, k, x]

    def stage2(s, k):
        for o in (1, 3, 2):
            enter(s, k, o, behind(o), behind(o), behind(o)).wait_recv()
        total = r1[s, k, 0].astype(F32)
        for j in range(1, PART):
            total = total + r1[s, k, j].astype(F32)
        rt[s, k] = total.astype(BF16)
        for o in FAR:
            to = (zl + o) % 4
            along(s, k, o, zl, to).start()
        rz[s, k, zl] = rt[s, k]

    def stage3(s, k):
        for o in (1, 3, 2):
            src = (zl + 4 - o) % 4
            along(s, k, o, src, src).wait_recv()
        total = jnp.zeros((HD, HD), F32)
        for n in range(4):
            counts = (zl > n) if s == 0 else (zl < n)
            total = total + jnp.where(counts, 1.0, 0.0) * rz[s, k, n].astype(F32)
        for j in range(4):
            n = j if s == 0 else 3 - j
            ex[s, k, n] = total.astype(BF16)
            total = total + r1[s, k, n].astype(F32)
        for o in FAR:
            leave(s, k, o, ahead(o), x, ahead(o)).start()
        pr[s, k, x] = ex[s, k, x]

    def stage4(s, k):
        for o in (1, 3, 2):
            leave(s, k, o, behind(o), behind(o), behind(o)).wait_recv()
        mine_on = (core if s == 0 else 1 - core).astype(F32)
        for j in range(PART):
            own = st[s, SPAN * k + PART * core + j].astype(F32)
            po[s, k, j] = (pr[s, k, j].astype(F32) + (1.0 - mine_on) * own).astype(BF16)
        pair_back(s, k, core).start()
        for j in range(PART):
            theirs = pb[s, k, j].astype(F32)
            si[s, SPAN * k + PART * core + j] = (pr[s, k, j].astype(F32) + mine_on * theirs).astype(BF16)

    def stage5(s, k):
        pair_back(s, k, other).wait_recv()

    slot = 2 * y + core

    def xrows(n):
        return pl.ds(pl.multiple_of(TOK * n, TOK), TOK)

    own_x = pltpu.make_async_copy(x_ref, xb.at[xrows(slot)], loc.at[0])

    def x_send(o):
        return remote(
            x_ref, xb.at[xrows(slot)], xb_s.at[o], xb_r.at[o],
            dev((y + o) % 4, zh, zl, x, core),
        )

    def x_in(o):
        src = (y + 4 - o) % 4
        return remote(
            x_ref, xb.at[xrows(2 * src + core)], xb_s.at[o], xb_r.at[o],
            dev(src, zh, zl, x, core),
        )

    def x_pass(o, who):
        rows = xb.at[xrows(2 * ((y + 4 - o) % 4) + who)]
        return remote(rows, rows, xb_s.at[4 + o], xb_r.at[4 + o], partner)

    x_keep = remote(x_ref, xb.at[xrows(slot)], xb_s.at[4], xb_r.at[4], partner)
    x_keep_in = remote(x_ref, xb.at[xrows(2 * y + other)], xb_s.at[4], xb_r.at[4], partner)

    def local_out(h):
        at_h = cols(h)
        s_h = mm(qf[:, at_h], kf[:, at_h], NT)
        s_h = jnp.where(causal, s_h, 0.0).astype(BF16)
        sc[h] = s_h
        ol[:, at_h] = mm(s_h, v_ref[:, at_h], NN)

    def grads(h):
        at_h = cols(h)
        out = ol[:, at_h] + mm(qf[:, at_h], si[0, h], NN)
        inv = lax.rsqrt(jnp.mean(out * out, axis=-1, keepdims=True) + EPS)
        normed = out * inv
        up = og_ref[:, at_h].astype(F32)
        proj = jnp.mean(up * normed, axis=-1, keepdims=True)
        g_h = (inv * (up - normed * proj)).astype(BF16)
        go[:, at_h] = g_h
        st[1, h] = mm(qf[:, at_h], g_h, TN).astype(BF16)

    def local_grads(h):
        at_h = cols(h)
        g_h = go[:, at_h]
        gs = mm(g_h, v_ref[:, at_h], NT)
        gs = jnp.where(causal, gs, 0.0).astype(BF16)
        total = mm(gs, kf[:, at_h], NN) + mm(g_h, si[0, h], NT)
        dq[:, at_h] = (total * slope(q_ref[:, at_h].astype(F32))).astype(BF16)
        dkl[:, at_h] = mm(gs, qf[:, at_h], TN)
        dvl[:, at_h] = mm(sc[h], g_h, TN)

    def last(h):
        at_h = cols(h)
        gi = si[1, h]
        total = dkl[:, at_h] + mm(v_ref[:, at_h], gi, NT)
        total = total * slope(k_ref[:, at_h].astype(F32))
        dk[:, at_h] = total.astype(BF16)
        kgt[pl.ds(pl.multiple_of(h * HD, HD), HD), :] = total.T.astype(BF16)
        dv[:, at_h] = (dvl[:, at_h] + mm(kf[:, at_h], gi, NN)).astype(BF16)

    def begin(k):
        heads(k, states)
        pair_out(0, k).start()

    def middle(k):
        stage5(0, k)
        heads(k, grads)
        pair_out(1, k).start()

    def end(k):
        stage5(1, k)
        heads(k, last)

    heads(0, states)
    pl.semaphore_wait(barrier, 17 + ((y - zl) * (y - zl) + 8) // 9)
    pair_out(0, 0).start()
    own_x.start()
    for o in FAR:
        x_send(o).start()
    begin(1)
    stage1(0, 0)
    begin(2)
    stage1(0, 1)
    stage1(0, 2)
    x_keep.start()
    heads(0, local_out)
    stage2(0, 0)
    heads(1, local_out)
    stage2(0, 1)
    heads(2, local_out)
    stage2(0, 2)
    stage3(0, 0)
    stage3(0, 1)
    stage4(0, 0)
    stage3(0, 2)
    stage4(0, 1)
    middle(0)
    stage4(0, 2)
    stage1(1, 0)
    middle(1)
    stage1(1, 1)
    stage2(1, 0)
    middle(2)
    stage1(1, 2)
    stage2(1, 1)
    heads(0, local_grads)
    stage3(1, 0)
    stage2(1, 2)
    heads(1, local_grads)
    stage3(1, 1)
    stage4(1, 0)
    stage3(1, 2)
    heads(2, local_grads)
    for o in (1, 3, 2):
        x_in(o).wait_recv()
        x_pass(o, core).start()
    out_q = pltpu.make_async_copy(dq, dq_out, loc.at[1])
    out_q.start()
    stage4(1, 1)
    end(0)
    stage4(1, 2)
    end(1)
    end(2)

    def at_rows(y_, core_, n):
        return kgt.at[pl.ds(pl.multiple_of(768 * y_ + 192 * n + 96 * core_, 96), 96)]

    def at_put(src, n):
        return at.at[pl.ds(96 * n, 96), pl.ds(pl.multiple_of(TOK * src, TOK), TOK)]

    def at_send(o, cc, n):
        y_ = (y + o) % 4
        cc_ = (core + cc) % 2
        return remote(
            at_rows(y_, cc_, n), at_put(slot, n), at_s.at[2 * o + cc, n], at_r.at[2 * o + cc, n],
            dev(y_, zh, zl, x, cc_),
        )

    def at_in(o, cc, n):
        y_ = (y + 4 - o) % 4
        cc_ = (core + cc) % 2
        return remote(
            at_rows(y, core, n), at_put(2 * y_ + cc_, n), at_s.at[2 * o + cc, n], at_r.at[2 * o + cc, n],
            dev(y_, zh, zl, x, cc_),
        )

    peers = [(o, cc) for o in (2, 1, 3, 0) for cc in (0, 1) if (o, cc) != (0, 0)]
    for o, cc in peers:
        for n in range(4):
            at_send(o, cc, n).start()
    for n in range(4):
        keep = pltpu.make_async_copy(at_rows(y, core, n), at_put(slot, n), loc.at[4 + n])
        keep.start()
    out_k = pltpu.make_async_copy(dk, dk_out, loc.at[2])
    out_v = pltpu.make_async_copy(dv, dv_out, loc.at[3])
    out_k.start()
    out_v.start()

    own_x.wait()
    x_keep_in.wait_recv()
    for o in (1, 3, 2):
        x_pass(o, other).wait_recv()
    for n in range(4):
        pltpu.make_async_copy(at_rows(y, core, n), at_put(slot, n), loc.at[4 + n]).wait()
        for o, cc in peers:
            at_in(o, cc, n).wait_recv()

    z = zh * 4 + zl

    def cx_send(o, n):
        return remote(cp.at[n, ahead(o)], xr.at[n, x], cx_s.at[o, n], cx_r.at[o, n], x_peer(ahead(o)))

    def cx_in(o, n):
        return remote(cp.at[n, behind(o)], xr.at[n, behind(o)], cx_s.at[o, n], cx_r.at[o, n], x_peer(behind(o)))

    def product(n, carry):
        to = (z + 1 + n) % 8
        tile = (to % 4) * 2 + to // 4
        out = mm(at[...], xb[:, pl.ds(pl.multiple_of(tile * 384, 384), 384)], NN).astype(BF16)
        for i in range(4):
            cp[n, i] = out[96 * i:96 * (i + 1), :]
        for o in FAR:
            cx_send(o, n).start()
        return carry

    lax.fori_loop(0, 8, product, 0)

    def z_send(n):
        to = (z + 1 + n) % 8
        return remote(
            zs.at[n], zr.at[n], z_s.at[n], z_r.at[n], dev(y, to // 4, to % 4, x, core),
        )

    def z_in(n):
        src = (z + 7 - n) % 8
        return remote(
            zs.at[n], zr.at[n], z_s.at[n], z_r.at[n], dev(y, src // 4, src % 4, x, core),
        )

    def sum_x(n):
        for o in (1, 3, 2):
            cx_in(o, n).wait_recv()
        total = cp[n, x].astype(F32)
        for o in range(1, 4):
            total = total + xr[n, (x + o) % 4].astype(F32)
        return total

    def relay(n, carry):
        zs[n] = sum_x(n).astype(BF16)
        z_send(n).start()
        return carry

    lax.fori_loop(0, 7, relay, 0)
    total = sum_x(7)
    for n in range(7):
        z_in(n).wait_recv()
        total = total + zr[n].astype(F32)
    tb[...] = total.astype(BF16)

    turn = remote(tb, tr, t_s.at[0], t_r.at[0], flip)

    @pl.when(off)
    def _():
        turn.start()
        turn.wait()
        dw_out[...] = tr[...].astype(F32) * SCALE

    @pl.when(jnp.logical_not(off))
    def _():
        dw_out[...] = tb[...].astype(F32) * SCALE

    for s in (0, 1):
        for k in range(CHUNKS):
            pair_out(s, k).wait_send()
            pair_back(s, k, core).wait_send()
            for o in FAR:
                enter(s, k, o, ahead(o), x, ahead(o)).wait_send()
                along(s, k, o, zl, (zl + o) % 4).wait_send()
                leave(s, k, o, ahead(o), x, ahead(o)).wait_send()
    for o in FAR:
        x_send(o).wait_send()
        x_pass(o, core).wait_send()
        for n in range(8):
            cx_send(o, n).wait_send()
    x_keep.wait_send()
    for o, cc in peers:
        for n in range(4):
            at_send(o, cc, n).wait_send()
    for n in range(7):
        z_send(n).wait_send()
    out_q.wait()
    out_k.wait()
    out_v.wait()


def hand_on(*refs):
    count = len(refs) // 2
    for source, target in zip(refs[:count], refs[count:]):
        target[...] = source[...]


def shards(layer_input, query_rows, key_rows, value_rows, out_grad):
    vmem = pl.BlockSpec(memory_space=pltpu.VMEM)
    hbm = pl.BlockSpec(memory_space=pl.ANY)
    rows = (TOK, WIDE)
    steps = (2, CHUNKS)
    square = (HD, HD)
    dma = pltpu.SemaphoreType.DMA
    dq, dk, dv, dw = pl.pallas_call(
        kernel,
        out_shape=(
            jax.ShapeDtypeStruct(rows, BF16),
            jax.ShapeDtypeStruct(rows, BF16),
            jax.ShapeDtypeStruct(rows, BF16),
            jax.ShapeDtypeStruct((96, 384), F32),
        ),
        in_specs=[hbm, vmem, vmem, vmem, vmem],
        out_specs=(hbm, hbm, hbm, vmem),
        scratch_shapes=[
            pltpu.VMEM(rows, BF16),
            pltpu.VMEM(rows, BF16),
            pltpu.VMEM(rows, BF16),
            pltpu.VMEM(rows, F32),
            pltpu.VMEM(rows, F32),
            pltpu.VMEM(rows, F32),
            pltpu.VMEM((HEADS, HD, HD), BF16),
            pltpu.VMEM((2, HEADS, HD, HD), BF16),
            pltpu.VMEM(steps + (PART,) + square, BF16),
            pltpu.VMEM(steps + (PART,) + square, BF16),
            pltpu.VMEM(steps + (PART,) + square, BF16),
            pltpu.VMEM(steps + square, BF16),
            pltpu.VMEM(steps + (PART,) + square, BF16),
            pltpu.VMEM(steps + (PART,) + square, BF16),
            pltpu.VMEM(steps + (PART,) + square, BF16),
            pltpu.VMEM(steps + (PART,) + square, BF16),
            pltpu.VMEM((2, HEADS, HD, HD), BF16),
            pltpu.VMEM(rows, BF16),
            pltpu.VMEM(rows, BF16),
            pltpu.VMEM(rows, BF16),
            pltpu.VMEM((WIDE, TOK), BF16),
            pltpu.VMEM((8 * TOK, WIDE), BF16),
            pltpu.VMEM((384, 8 * TOK), BF16),
            pltpu.VMEM((8, 4, 96, 384), BF16),
            pltpu.VMEM((8, 4, 96, 384), BF16),
            pltpu.VMEM((8, 96, 384), BF16),
            pltpu.VMEM((8, 96, 384), BF16),
            pltpu.VMEM((96, 384), BF16),
            pltpu.VMEM((96, 384), BF16),
            dma((2, 2, CHUNKS)), dma((2, 2, CHUNKS)),
            dma(steps + (4,)), dma(steps + (4,)),
            dma(steps + (4,)), dma(steps + (4,)),
            dma(steps + (4,)), dma(steps + (4,)),
            dma((8,)), dma((8,)),
            dma((8, 4)), dma((8, 4)),
            dma((4, 8)), dma((4, 8)),
            dma((8,)), dma((8,)),
            dma((1,)), dma((1,)),
            dma((8,)),
        ],
        compiler_params=pltpu.CompilerParams(
            collective_id=0, has_side_effects=True, vmem_limit_bytes=60 * 1024 * 1024
        ),
    )(layer_input[0], query_rows[0], key_rows[0], value_rows[0], out_grad[0])
    blocks = [pl.BlockSpec((32, WIDE), lambda i: (i, 0))] * 3 + [pl.BlockSpec((24, 384), lambda i: (i, 0))]
    arrays = (dq, dk, dv, dw)
    dq, dk, dv, dw = pl.pallas_call(
        hand_on,
        out_shape=tuple(jax.ShapeDtypeStruct(a.shape, a.dtype) for a in arrays),
        grid=(4,),
        in_specs=blocks,
        out_specs=tuple(blocks),
    )(*arrays)
    return dq[None], dk[None], dv[None], dw


def solution(mesh):
    placed = (P("dp", "ctx", None),) * 5
    return jax.shard_map(
        shards,
        mesh=mesh,
        in_specs=placed,
        out_specs=(
            P("dp", "ctx", None),
            P("dp", "ctx", None),
            P("dp", "ctx", None),
            P("ctx", "dp"),
        ),
        check_vma=False,
    )
```
